32 devices in a mesh: groups: 2 (over x), ctx: 16 (over z, y, core).
Axes of the slice: x: 2, y: 2, z: 4, core: 2. Of those that a mesh axis runs over, the one named last changes fastest.
Arguments:
- q_in: bfloat16 [8192, 4096], P(('groups', 'ctx')), parts along dimension 0, may hold values from -6 to 6
- k_in: bfloat16 [8192, 4096], P(('groups', 'ctx')), parts along dimension 0, may hold values from -6 to 6
- v_in: bfloat16 [8192, 4096], P(('groups', 'ctx')), parts along dimension 0, may hold values from -6 to 6
- conv_filter: float32 [3, 7, 4096], replicated, may hold values from -2 to 2
- decay_rate: float32 [256, 16], replicated, may hold values from 2.4414063e-05 to 0.133333333, as said below
- residue: float32 [256, 16], replicated, may hold values from -0.387298335 to 0.387298335
- genome_lengths: int32 [8], P('groups'), parts along dimension 0, may hold values from 1 to 2048, as said below
Outputs:
- gated: bfloat16 [8192, 4096], P(('groups', 'ctx')), parts along dimension 0
The draws below stay inside these ranges and needn't reach their ends.
There are 2 independent parts, one for each index of `groups`. The reference program is written for one: setup_inputs(seed, part) draws one part's arguments, and reference() takes and returns one part's arrays. A program takes and returns all parts, laid end to end along the dimension named above; an argument that names none is the same for every part. Nothing has to cross between parts.
Inputs may be any that keep to these rules, and one draw needn't show every extreme that they name: `decay_rate`: positive rates. `genome_lengths`: positive lengths that sum to 4096; one genome holds exactly 2048 bases.
All inputs are finite; a program needn't handle non-finite values.
Results may differ from the reference program's by a relative error of at most 0.0065.
Values may be sent and summed in bfloat16 or wider, within the bound.
No kernel may reach another device: no remote copies, remote signals or barrier semaphores. Data moves between devices by JAX's collectives and lax.ppermute only.
A program may use at most 128 MiB of HBM per device.

```python
import jax
import jax.numpy as jnp
from jax import lax

D = 4096
CPG = 16
POLES = 16
TAPS = 7
TOTAL = 4096
FILTERS = 256


def modal_pair(key):
    flag_key = jax.random.fold_in(key, 101)
    fast_key = jax.random.fold_in(key, 102)
    slow_key = jax.random.fold_in(key, 103)
    resid_key = jax.random.fold_in(key, 104)
    share = 0.5
    fast_flag = jax.random.uniform(flag_key, (FILTERS, 1), jnp.float32) < share
    fast = 1.0 / 50.0 * jnp.exp(jax.random.uniform(fast_key, (FILTERS, POLES), jnp.float32) * jnp.log(200.0 / 30.0))
    slow = jnp.exp(jax.random.uniform(slow_key, (FILTERS, POLES), jnp.float32, jnp.log(0.1), jnp.log(2.0))) / TOTAL
    rates = jnp.where(fast_flag, fast, slow)
    base = jnp.clip(jax.random.normal(resid_key, (FILTERS, POLES), jnp.float32), -3.0, 3.0)
    residues = base * jnp.sqrt(2.0 * rates / POLES)
    return (rates, residues)


def draw_decay_rate(key, part):
    return modal_pair(key)[0].astype(jnp.float32)


def draw_residue(key, part):
    return modal_pair(key)[1].astype(jnp.float32)


def draw_genome_lengths(key, part):
    largest = TOTAL // 2
    remain = TOTAL - largest
    first_cut = jax.random.randint(jax.random.fold_in(key, 201), (), 1, remain, dtype=jnp.int32)
    second_cut = jax.random.randint(jax.random.fold_in(key, 202), (), 1, remain - 1, dtype=jnp.int32)
    second_cut = second_cut + (second_cut >= first_cut).astype(jnp.int32)
    lower_cut = jnp.minimum(first_cut, second_cut)
    upper_cut = jnp.maximum(first_cut, second_cut)
    pieces = jnp.stack([lower_cut, upper_cut - lower_cut, remain - upper_cut]).astype(jnp.int32)
    big_slot = jax.random.randint(jax.random.fold_in(key, 203), (), 0, 4, dtype=jnp.int32)
    slot_index = jnp.arange(4, dtype=jnp.int32)
    piece_index = jnp.clip(slot_index - (slot_index > big_slot).astype(jnp.int32), 0, 2)
    picked = jnp.take(pieces, piece_index)
    return jnp.where(slot_index == big_slot, jnp.int32(largest), picked).astype(jnp.int32)


def steps_of(key, shape, split, smallest, high):
    level, own = 1.0, jax.random.fold_in(key, 6)
    for position, blocks in split:
        steps = jnp.exp(jax.random.uniform(jax.random.fold_in(own, position), (blocks,), jnp.float32, smallest / len(split), high / len(split)))
        level = level * jnp.repeat(steps, shape[position] // blocks).reshape([-1 if axis == position else 1 for axis in range(len(shape))])
    return level


def noise(key, dims, deviation, most, cuts=(), kind=jnp.bfloat16):
    factor_of = steps_of(key, dims, cuts, -0.22, 0.18) if cuts else 1.0
    drawn = jax.random.normal(key, dims, jnp.float32) * deviation * factor_of
    return jnp.minimum(jnp.maximum(drawn, -most), most).astype(kind)


def setup_inputs(seed: int = 0, part: int = 0) -> dict:
    arg_keys = jax.random.split(jax.random.key(seed), 8)
    own_keys = jax.random.split(jax.random.fold_in(arg_keys[7], part), 8)
    return {
        "q_in": noise(own_keys[0], (TOTAL, D), 1.0, 6.0, ((0, 16),)),
        "k_in": noise(own_keys[1], (TOTAL, D), 1.0, 6.0, ((0, 16),)),
        "v_in": noise(own_keys[2], (TOTAL, D), 1.0, 6.0, ((0, 16),)),
        "conv_filter": noise(arg_keys[3], (3, TAPS, D), TAPS ** -0.5, 2.0, (), jnp.float32),
        "decay_rate": draw_decay_rate(jax.random.fold_in(arg_keys[7], 71), part),
        "residue": draw_residue(jax.random.fold_in(arg_keys[7], 71), part),
        "genome_lengths": draw_genome_lengths(jax.random.fold_in(jax.random.fold_in(arg_keys[7], part), 71), part),
    }


def segment_ids(genome_lengths, positions):
    starts = jnp.cumsum(genome_lengths) - genome_lengths
    return jnp.sum((starts[None, :] <= positions[:, None]).astype(jnp.int32), axis=1)


def short_conv(stream, taps, segments, total_rows):
    source = stream.astype(jnp.float32)
    result = jnp.zeros(source.shape, jnp.float32)
    for offset_tap in range(TAPS):
        moved = jnp.pad(source, ((offset_tap, 0), (0, 0)))[:total_rows]
        moved_ids = jnp.pad(segments, (offset_tap, 0), constant_values=-1)[:total_rows]
        keep = (moved_ids == segments).astype(jnp.float32)
        result = result + taps[offset_tap][None, :] * moved * keep[:, None]
    return result.astype(jnp.bfloat16)


def reference(q_in, k_in, v_in, conv_filter, decay_rate, residue, genome_lengths):
    total_rows = q_in.shape[0]
    positions = jnp.arange(total_rows, dtype=jnp.int32)
    segments = segment_ids(genome_lengths, positions)
    query = short_conv(q_in, conv_filter[0], segments, total_rows)
    keyed = short_conv(k_in, conv_filter[1], segments, total_rows)
    valued = short_conv(v_in, conv_filter[2], segments, total_rows)
    mixed = keyed.astype(jnp.float32) * valued.astype(jnp.float32)
    decay = jnp.repeat(jnp.exp(-decay_rate).T, CPG, axis=1)
    weights = jnp.repeat(residue.T, CPG, axis=1)
    earlier_ids = jnp.pad(segments, (1, 0), constant_values=-1)[:total_rows]
    keep_state = (earlier_ids == segments).astype(jnp.float32)

    def advance(state, inputs):
        row_in, keep_row = inputs
        state = decay * state * keep_row + row_in[None, :]
        return state, jnp.sum(weights * state, axis=0)

    start_state = jnp.zeros((POLES, q_in.shape[1]), jnp.float32)
    _, filtered = lax.scan(advance, start_state, (mixed, keep_state))
    return (query.astype(jnp.float32) * filtered).astype(jnp.bfloat16)
```

```python
import functools

import jax
import jax.numpy as jnp
from jax import lax
from jax.experimental import pallas as pl
from jax.experimental.pallas import tpu as pltpu
from jax.sharding import PartitionSpec as P

CPG = 16
POLES = 16
TAPS = 7
LANES = 128
UNIT = 16
F32 = jnp.float32
BF16 = jnp.bfloat16


def roll(value, steps):
    return pltpu.roll(value, steps, 0)


def conv_rows(x, taps, before, row, masks=None):
    b1, b2, b_low, b_mid = before
    r1, r2 = roll(x, 1), roll(x, 2)
    low = taps[6] * x
    r_low = roll(low, 3)
    a1 = jnp.where(row < 1, b1, r1)
    a2 = jnp.where(row < 2, b2, r2)
    s_low = jnp.where(row < 3, b_low, r_low)
    if masks is not None:
        a1 = jnp.where(masks[0], a1, 0.0)
        a2 = jnp.where(masks[1], a2, 0.0)
        s_low = jnp.where(masks[2], s_low, 0.0)
    mid = taps[3] * x + taps[4] * a1 + (taps[5] * a2 + s_low)
    r_mid = roll(mid, 3)
    s_mid = jnp.where(row < 3, b_mid, r_mid)
    if masks is not None:
        s_mid = jnp.where(masks[2], s_mid, 0.0)
    out = taps[0] * x + taps[1] * a1 + (taps[2] * a2 + s_mid)
    return out, (r1, r2, r_low, r_mid)


def no_rows():
    zero = jnp.zeros((8, LANES), F32)
    return (zero, zero, zero, zero)


def rounded(value):
    return value.astype(BF16).astype(F32)


def features_kernel(
    starts, q_ref, k_ref, v_ref, halo_ref, taps_ref, lam_ref, res_ref,
    query_ref, local_ref, span_ref, xs, ys, *, rows, genomes,
):
    tiles = q_ref.shape[1] // LANES
    row = lax.broadcasted_iota(jnp.int32, (8, LANES), 0)
    streams = (q_ref, k_ref, v_ref)

    def tap_rows(stream, lanes):
        return [
            jnp.broadcast_to(taps_ref[stream, j : j + 1, lanes], (8, LANES)) for j in range(TAPS)
        ]

    def emit(tile, lanes, unit_row, q_pair, k_pair, v_pair):
        query_ref[pl.ds(unit_row, UNIT), lanes] = jnp.concatenate(q_pair, 0).astype(BF16)
        mixed = jnp.concatenate(
            [rounded(k) * rounded(v) for k, v in zip(k_pair, v_pair)], 0
        )
        xs[pl.ds(pl.multiple_of(tile * rows + unit_row, UNIT), UNIT), :] = mixed

    def tile_body(tile, _):
        lanes = pl.ds(pl.multiple_of(tile * LANES, LANES), LANES)
        taps = [tap_rows(s, lanes) for s in range(3)]
        carry = []
        for s in range(3):
            halo = halo_ref[s, :, lanes].astype(F32)
            carry.append(conv_rows(halo, taps[s], no_rows(), row)[1])
        for unit in range(rows // UNIT):
            pairs = []
            for s in range(3):
                x16 = streams[s][unit * UNIT : (unit + 1) * UNIT, lanes].astype(F32)
                y0, c = conv_rows(x16[:8], taps[s], carry[s], row)
                y1, c = conv_rows(x16[8:], taps[s], c, row)
                carry[s] = c
                pairs.append((y0, y1))
            emit(tile, lanes, unit * UNIT, *pairs)
        return 0

    lax.fori_loop(0, tiles, tile_body, 0)

    def patch(unit):
        unit_row = pl.multiple_of(unit * UNIT, UNIT)
        above = pl.multiple_of(jnp.maximum(unit - 1, 0) * UNIT, UNIT)

        def masks_at(first):
            at = first + row
            out = []
            for reach in (1, 2, 3):
                bad = jnp.zeros((8, LANES), jnp.bool_)
                for g in range(genomes):
                    bad = bad | ((at >= starts[g]) & (at < starts[g] + reach))
                out.append(jnp.logical_not(bad))
            return out

        masks = [masks_at(unit_row - 8), masks_at(unit_row), masks_at(unit_row + 8)]

        def patch_tile(tile, _):
            lanes = pl.ds(pl.multiple_of(tile * LANES, LANES), LANES)
            pairs = []
            for s in range(3):
                taps = tap_rows(s, lanes)
                halo = halo_ref[s, :, lanes].astype(F32)
                prev = streams[s][pl.ds(above, UNIT), lanes].astype(F32)[8:]
                prev = jnp.where(unit == 0, halo, prev)
                x16 = streams[s][pl.ds(unit_row, UNIT), lanes].astype(F32)
                c = conv_rows(prev, taps, no_rows(), row, masks[0])[1]
                y0, c = conv_rows(x16[:8], taps, c, row, masks[1])
                y1, c = conv_rows(x16[8:], taps, c, row, masks[2])
                pairs.append((y0, y1))
            emit(tile, lanes, unit_row, *pairs)
            return 0

        lax.fori_loop(0, tiles, patch_tile, 0)

    for g in range(genomes):
        start = starts[g]
        first = jnp.maximum(start, 0) // UNIT
        last = jnp.minimum(start + TAPS - 2, rows - 1) // UNIT
        near = (start > 1 - TAPS) & (start < rows)

        @pl.when(near)
        def _():
            patch(first)

        @pl.when(near & (last != first))
        def _():
            patch(last)

    decay = [jnp.exp(-lam_ref[n]) for n in range(POLES)]
    weight = [res_ref[n] for n in range(POLES)]

    def steps(first, state, keeps):
        state = list(state)
        for r in range(8):
            x = xs[pl.ds(first + r, tiles, stride=rows), :]
            parts = []
            for n in range(POLES):
                old = state[n] if keeps is None else state[n] * keeps[r]
                state[n] = decay[n] * old + x
                parts.append(weight[n] * state[n])
            while len(parts) > 1:
                parts = [a + b for a, b in zip(parts[::2], parts[1::2])]
            ys[pl.ds(first + r, tiles, stride=rows), :] = parts[0]
        return tuple(state)

    def eight(i, state):
        first = pl.multiple_of(i * 8, 8)
        cut = functools.reduce(
            jnp.logical_or,
            [(starts[g] >= first) & (starts[g] < first + 8) for g in range(genomes)],
        )

        def broken(state):
            keeps = []
            for r in range(8):
                here = functools.reduce(
                    jnp.logical_or, [starts[g] == first + r for g in range(genomes)]
                )
                keeps.append(jnp.where(here, 0.0, 1.0))
            return steps(first, state, keeps)

        return lax.cond(cut, broken, lambda s: steps(first, s, None), state)

    zero = jnp.zeros((tiles, LANES), F32)
    final = lax.fori_loop(0, rows // 8, eight, (zero,) * POLES)
    for n in range(POLES):
        span_ref[n] = final[n]
    for tile in range(tiles):
        local_ref[:, tile * LANES : (tile + 1) * LANES] = ys[tile * rows : (tile + 1) * rows, :]


def gate_kernel(
    starts, core_ref, local_ref, query_ref, mine_ref, other_ref, lam_ref, res_ref, out_ref,
    *, rows, genomes,
):
    group = pl.program_id(0)
    tiles = 2 * LANES // LANES
    half = pl.num_programs(0) // 2
    use_mine = (group // half) == core_ref[0]
    first = (group % half) * tiles
    pieces = []
    for t in range(tiles):
        at = pl.ds(first + t, POLES, stride=half * tiles)
        pieces.append(jnp.where(use_mine, mine_ref[at, :], other_ref[at, :]))
    state = jnp.concatenate(pieces, 1)
    width = state.shape[1]
    filters = width // CPG
    lane_filter = lax.broadcasted_iota(jnp.int32, (POLES, width), 1) // CPG
    hi = state.astype(BF16)
    lo = (state - hi.astype(F32)).astype(BF16)

    def spread(value):
        wide = value.astype(F32)
        return jnp.concatenate(
            [jnp.where(lane_filter == f, wide, 0.0).astype(BF16) for f in range(filters)], 0
        )

    s_hi, s_lo = spread(hi), spread(lo)
    t = lax.broadcasted_iota(jnp.int32, (rows, width), 0)
    keep = jnp.ones((rows, width), jnp.bool_)
    for g in range(genomes):
        keep = keep & jnp.logical_not((starts[g] >= 0) & (t >= starts[g]))
    power = res_ref[0] * jnp.exp(-lam_ref[0] * (t + 1).astype(F32))
    power = jnp.where(keep, power, 0.0)
    e_hi = power.astype(BF16)
    e_lo = (power - e_hi.astype(F32)).astype(BF16)
    dot = functools.partial(jnp.dot, preferred_element_type=F32)
    filtered = local_ref[...] + dot(e_hi, s_hi) + (dot(e_lo, s_hi) + dot(e_hi, s_lo))
    out_ref[...] = (query_ref[...].astype(F32) * filtered).astype(BF16)


def exchange(value, pairs):
    return lax.ppermute(value, "ctx", pairs)


def per_device(q_in, k_in, v_in, conv_filter, decay_rate, residue, genome_lengths):
    rows, width = q_in.shape
    filters = width // CPG
    tiles = width // LANES
    genomes = genome_lengths.shape[0]
    count = lax.axis_size("ctx")
    index = lax.axis_index("ctx")
    starts = jnp.cumsum(genome_lengths) - genome_lengths
    relative = (starts - index * rows).astype(jnp.int32)

    tail = jnp.stack([q_in[rows - 8 :], k_in[rows - 8 :], v_in[rows - 8 :]])
    halo = exchange(tail, [(i, i + 1) for i in range(count - 1)])

    lam_wide = jnp.repeat(decay_rate.T, CPG, axis=1).reshape(POLES, tiles, LANES)
    res_wide = jnp.repeat(residue.T, CPG, axis=1).reshape(POLES, tiles, LANES)

    block = 8 * LANES
    stream_spec = pl.BlockSpec((rows, block), lambda b, *_: (0, b))
    wide_spec = pl.BlockSpec((POLES, 8, LANES), lambda b, *_: (0, b, 0))
    query, local, span = pl.pallas_call(
        functools.partial(features_kernel, rows=rows, genomes=genomes),
        grid_spec=pltpu.PrefetchScalarGridSpec(
            num_scalar_prefetch=1,
            grid=(width // block,),
            in_specs=[
                stream_spec, stream_spec, stream_spec,
                pl.BlockSpec((3, 8, block), lambda b, *_: (0, 0, b)),
                pl.BlockSpec((3, TAPS, block), lambda b, *_: (0, 0, b)),
                wide_spec, wide_spec,
            ],
            out_specs=[stream_spec, stream_spec, wide_spec],
            scratch_shapes=[
                pltpu.VMEM((8 * rows, LANES), F32),
                pltpu.VMEM((8 * rows, LANES), F32),
            ],
        ),
        out_shape=[
            jax.ShapeDtypeStruct((rows, width), BF16),
            jax.ShapeDtypeStruct((rows, width), F32),
            jax.ShapeDtypeStruct((POLES, tiles, LANES), F32),
        ],
        name="features",
    )(relative, q_in, k_in, v_in, halo, conv_filter, lam_wide, res_wide)

    def end_id(device):
        return jnp.sum((starts <= (device + 1) * rows - 1).astype(jnp.int32))

    def joined(a, b):
        return (end_id(a) == end_id(b)).astype(F32)

    core = index % 2
    half = tiles // 2
    lam_mine = lax.dynamic_slice_in_dim(lam_wide, core * half, half, 1)

    def power(devices):
        return jnp.exp(-lam_mine * (rows * devices).astype(F32))

    one = jnp.int32(1)
    away = [(i, i ^ 1) for i in range(count)]
    given = lax.dynamic_slice_in_dim(span, (1 - core) * half, half, 1)
    own = lax.dynamic_slice_in_dim(span, core * half, half, 1)
    got = exchange(given, away)
    left = jnp.where(core == 0, own, got)
    right = jnp.where(core == 0, got, own)
    chip_first = index - core
    total = power(one) * joined(chip_first, chip_first + 1) * left + right
    prefix = jnp.zeros_like(total)
    size = 2
    while size < count:
        other = exchange(total, [(i, i ^ size) for i in range(count)])
        is_right = (index // size) % 2 == 1
        block_first = index // size * size
        block_last = block_first + size - 1
        before = block_first - 1
        into = power(chip_first - block_first) * joined(before, chip_first - 1) * other
        prefix = prefix + jnp.where(is_right, into, 0.0)
        gain = power(jnp.int32(size))
        as_right = gain * joined(before, block_last) * other + total
        as_left = gain * joined(block_last, block_last + size) * total + other
        total = jnp.where(is_right, as_right, as_left)
        size *= 2
    second = power(one) * joined(chip_first - 1, chip_first) * prefix + left
    mine = jnp.where(core == 0, prefix, second)
    others = jnp.where(core == 0, second, prefix)
    back = exchange(others, away)

    groups = filters // 16
    lane_spec = pl.BlockSpec((rows, 2 * LANES), lambda b, *_: (0, b))
    flat_spec = pl.BlockSpec((1, 1, 2 * LANES), lambda b, *_: (b, 0, 0))
    whole = pl.BlockSpec((POLES * half, LANES), lambda b, *_: (0, 0))
    return pl.pallas_call(
        functools.partial(gate_kernel, rows=rows, genomes=genomes),
        grid_spec=pltpu.PrefetchScalarGridSpec(
            num_scalar_prefetch=2,
            grid=(groups,),
            in_specs=[lane_spec, lane_spec, whole, whole, flat_spec, flat_spec],
            out_specs=lane_spec,
        ),
        out_shape=jax.ShapeDtypeStruct((rows, width), BF16),
        name="gate",
    )(
        relative, jnp.reshape(core, (1,)).astype(jnp.int32), local, query,
        mine.reshape(POLES * half, LANES), back.reshape(POLES * half, LANES),
        decay_rate.reshape(groups, 1, 2 * LANES), residue.reshape(groups, 1, 2 * LANES),
    )


def solution(mesh):
    in_specs = (
        P(("groups", "ctx"), None),
        P(("groups", "ctx"), None),
        P(("groups", "ctx"), None),
        P(),
        P(),
        P(),
        P("groups"),
    )
    return jax.shard_map(
        per_device, mesh=mesh, in_specs=in_specs, out_specs=P(("groups", "ctx"), None), check_vma=False
    )
```

```python
import functools

import jax
import jax.numpy as jnp
from jax import lax
from jax.experimental import pallas as pl
from jax.experimental.pallas import tpu as pltpu
from jax.sharding import PartitionSpec as P

CPG = 16
POLES = 16
TAPS = 7
LANES = 128
UNIT = 16
GROUP = LANES // CPG
F32 = jnp.float32
BF16 = jnp.bfloat16


def iota(shape, axis):
    return lax.broadcasted_iota(jnp.int32, shape, axis)


def lanes_of(tile):
    if isinstance(tile, int):
        return slice(tile * LANES, (tile + 1) * LANES)
    return pl.ds(pl.multiple_of(tile * LANES, LANES), LANES)


def split(value):
    hi = value.astype(BF16)
    return hi, (value - hi.astype(F32)).astype(BF16)


def any_of(flags):
    return functools.reduce(jnp.logical_or, flags)


def conv_terms(taps, window):
    terms = [taps[j] * window(j) for j in range(TAPS)]
    even = (terms[0] + terms[1]) + (terms[2] + terms[3])
    return even + ((terms[4] + terms[5]) + terms[6])


def short_conv(starts, streams, halo_refs, taps_refs, xs, emit, tiles, rows, genomes):
    count = len(streams)
    cut_above = functools.reduce(
        jnp.maximum, [jnp.where(starts[g] <= 0, starts[g], -rows) for g in range(genomes)]
    )
    halo_kept = iota((8, LANES), 0) - 8 >= cut_above

    def base(tile, _):
        lanes = lanes_of(tile)
        for s in range(count):
            xs[s, tile, :8] = jnp.where(halo_kept, halo_refs[s][:, lanes].astype(F32), 0.0)
            xs[s, tile, 8:] = streams[s][:, lanes].astype(F32)
        taps = [
            [jnp.broadcast_to(taps_refs[s][j : j + 1, lanes], (8, LANES)) for j in range(TAPS)]
            for s in range(count)
        ]
        for r in range(0, rows, UNIT):
            done = []
            for s in range(count):
                for at in (r + 8, r + 16):
                    done.append(
                        conv_terms(
                            taps[s], lambda j, s=s, at=at: xs[s, tile, at - j : at - j + 8]
                        )
                    )
            emit(tile, lanes, r, done)
        return 0

    lax.fori_loop(0, tiles, base, 0)

    def patch(unit):
        first = pl.multiple_of(unit * UNIT, UNIT)
        cuts = []
        for h in range(2):
            at = first + 8 * h + iota((8, LANES), 0)
            cuts.append(
                [
                    any_of([(at >= starts[g]) & (at < starts[g] + j) for g in range(genomes)])
                    for j in range(1, TAPS)
                ]
            )

        def patch_tile(tile, _):
            lanes = lanes_of(tile)
            done = []
            for s in range(count):
                taps = [taps_refs[s][j : j + 1, lanes] for j in range(TAPS)]
                for h in range(2):

                    def window(j, s=s, h=h):
                        moved = xs[s, tile, pl.ds(first + 8 * (h + 1) - j, 8)]
                        return moved if j == 0 else jnp.where(cuts[h][j - 1], 0.0, moved)

                    done.append(conv_terms(taps, window))
            emit(tile, lanes, first, done)
            return 0

        lax.fori_loop(0, tiles, patch_tile, 0)

    for g in range(genomes):
        start = starts[g]
        inside = (start > 0) & (start < rows)
        unit = start // UNIT
        end = jnp.minimum(start + TAPS - 2, rows - 1) // UNIT

        @pl.when(inside)
        def _():
            patch(unit)

        @pl.when(inside & (end != unit))
        def _():
            patch(end)


def expand_kernel(lam_ref, res_ref, lam_rows, res_rows, lam_wide, *, tiles):
    parts = []
    for source in (lam_ref, res_ref):
        rest = source[...]
        for _ in range(3):
            part = rest.astype(BF16)
            rest = rest - part.astype(F32)
            parts.append(part)
    parts = jnp.concatenate(parts, 0)
    for pair in range(tiles // 2):
        first = pair * 2 * GROUP
        side = first // LANES * LANES
        shape = (LANES, 2 * LANES)
        pick = iota(shape, 1) // CPG + (first - side) == iota(shape, 0)
        wide = jnp.dot(
            parts[:, side : side + LANES], jnp.where(pick, 1.0, 0.0).astype(BF16),
            preferred_element_type=F32,
        )
        wide = [wide[i * POLES : (i + 1) * POLES] for i in range(6)]
        lam = wide[0] + wide[1] + wide[2]
        res = wide[3] + wide[4] + wide[5]
        lam_wide[:, 2 * pair * LANES : (2 * pair + 2) * LANES] = lam
        for t in range(2):
            lam_rows[:, 2 * pair + t, :] = lam[:, lanes_of(t)]
            res_rows[:, 2 * pair + t, :] = res[:, lanes_of(t)]


def states_kernel(
    starts, k_ref, v_ref, k_halo, v_halo, taps_ref, lam_ref, res_ref,
    local_ref, span_ref, xs, mixed, final, *, rows, genomes,
):
    tiles = k_ref.shape[1] // LANES

    def emit(tile, lanes, first, done):
        k0, k1, v0, v1 = (value.astype(BF16).astype(F32) for value in done)
        row = pl.ds(pl.multiple_of(tile * 8, 8), 8)
        mixed[first // 8, row, :] = k0 * v0
        mixed[first // 8 + 1, row, :] = k1 * v1

    short_conv(
        starts, (k_ref, v_ref), (k_halo.at[0], v_halo.at[0]), (taps_ref.at[1], taps_ref.at[2]),
        xs, emit, tiles, rows, genomes,
    )
    decay = [jnp.exp(-lam_ref[n]) for n in range(POLES)]
    weight = [res_ref[n] for n in range(POLES)]

    def one(eight, r, state, keep=None):
        x = mixed[eight, pl.ds(r, tiles, stride=8), :]
        out, sums = [], [None, None]
        for n in range(POLES):
            old = state[n] if keep is None else state[n] * keep
            new = decay[n] * old + x
            term = weight[n] * new
            sums[n % 2] = term if sums[n % 2] is None else sums[n % 2] + term
            out.append(new)
        local_ref[eight, pl.ds(r, tiles, stride=8), :] = sums[0] + sums[1]
        return out

    size = 32

    def block(i, state):
        first = i * size
        cut = any_of(
            [(starts[g] > 0) & (starts[g] >= first) & (starts[g] < first + size) for g in range(genomes)]
        )

        def smooth(state):
            state = list(state)
            for r in range(size):
                state = one(i * (size // 8) + r // 8, r % 8, state)
            return tuple(state)

        def broken(state):
            def step(t, state):
                here = any_of([starts[g] == first + t for g in range(genomes)])
                keep = jnp.where(here, 0.0, 1.0)
                return tuple(one(i * (size // 8) + t // 8, t % 8, list(state), keep))

            return lax.fori_loop(0, size, step, state, unroll=8)

        return lax.cond(cut, broken, smooth, state)

    zero = jnp.zeros((tiles, LANES), F32)
    state = lax.fori_loop(0, rows // size, block, (zero,) * POLES)
    for n in range(POLES):
        final[n * tiles : (n + 1) * tiles, :] = state[n]
    for tile in range(tiles):
        span_ref[:, lanes_of(tile)] = final[pl.ds(tile, POLES, stride=tiles), :]


def query_kernel(starts, q_ref, q_halo, taps_ref, query_ref, xs, *, rows, genomes):
    def emit(tile, lanes, first, done):
        query_ref[pl.ds(first, UNIT), lanes] = jnp.concatenate(done, 0).astype(BF16)

    short_conv(
        starts, (q_ref,), (q_halo.at[0],), (taps_ref.at[0],), xs, emit,
        q_ref.shape[1] // LANES, rows, genomes,
    )


def gate_kernel(
    starts, core_ref, local_ref, query_ref, mine_ref, other_ref, lam_ref, res_ref, out_ref,
    *, rows, genomes,
):
    width = 2 * LANES
    filters = width // CPG
    use_mine = (pl.program_id(0) // (pl.num_programs(0) // 2)) == core_ref[0]
    lane_filter = iota((POLES, width), 1) // CPG
    t = iota((rows, width), 0)
    keep = jnp.logical_not(any_of([(starts[g] >= 0) & (t >= starts[g]) for g in range(genomes)]))
    ahead = jnp.where(keep, (t + 1).astype(F32), 1e9)
    dot = functools.partial(jnp.dot, preferred_element_type=F32)

    def spread(value):
        zero = jnp.zeros((), BF16)
        return jnp.concatenate(
            [jnp.where(lane_filter == f, value, zero) for f in range(filters)], 0
        )

    for group in range(out_ref.shape[1] // width):
        lanes = slice(group * width, (group + 1) * width)
        state = jnp.where(use_mine, mine_ref[:, lanes], other_ref[:, lanes])
        hi, lo = split(state)
        s_hi, s_lo = spread(hi), spread(lo)
        e_hi, e_lo = split(res_ref[group] * jnp.exp(-lam_ref[group] * ahead))
        carried = dot(e_hi, s_hi) + (dot(e_lo, s_hi) + dot(e_hi, s_lo))
        local = jnp.concatenate(
            [
                local_ref[:, (2 * group + t) * 8 : (2 * group + t + 1) * 8, :].reshape(rows, LANES)
                for t in range(2)
            ],
            1,
        )
        filtered = local + carried
        out_ref[:, lanes] = (query_ref[:, lanes].astype(F32) * filtered).astype(BF16)


def exchange(value, pairs):
    return lax.ppermute(value, "ctx", pairs)


def per_device(q_in, k_in, v_in, conv_filter, decay_rate, residue, genome_lengths):
    rows, width = q_in.shape
    tiles = width // LANES
    genomes = genome_lengths.shape[0]
    count = lax.axis_size("ctx")
    index = lax.axis_index("ctx")
    order = jnp.arange(genomes)
    starts = jnp.sum(jnp.where(order[None, :] < order[:, None], genome_lengths[None, :], 0), 1)
    relative = (starts - index * rows).astype(jnp.int32)

    tail = jnp.stack([x[rows - 8 :] for x in (q_in, k_in, v_in)])
    halo = exchange(tail, [(i, i + 1) for i in range(count - 1)])

    block = 8 * LANES
    steps = width // block
    stream = pl.BlockSpec((rows, block), lambda b, *_: (0, b))
    taps_spec = pl.BlockSpec((3, TAPS, block), lambda b, *_: (0, 0, b))
    row_spec = pl.BlockSpec((POLES, 8, LANES), lambda b, *_: (0, b, 0))
    local_spec = pl.BlockSpec((rows // 8, 8 * 8, LANES), lambda b, *_: (0, b, 0))
    local_shape = jax.ShapeDtypeStruct((rows // 8, tiles * 8, LANES), F32)

    def halo_spec(s):
        return pl.BlockSpec((1, 8, block), lambda b, *_: (s, 0, b))

    lam_rows, res_rows, lam_wide = pl.pallas_call(
        functools.partial(expand_kernel, tiles=tiles),
        out_shape=[
            jax.ShapeDtypeStruct((POLES, tiles, LANES), F32),
            jax.ShapeDtypeStruct((POLES, tiles, LANES), F32),
            jax.ShapeDtypeStruct((POLES, width), F32),
        ],
        name="expand",
        cost_estimate=pl.CostEstimate(flops=10**9, bytes_accessed=10**6, transcendentals=0),
    )(decay_rate.T, residue.T)

    local, span = pl.pallas_call(
        functools.partial(states_kernel, rows=rows, genomes=genomes),
        grid_spec=pltpu.PrefetchScalarGridSpec(
            num_scalar_prefetch=1,
            grid=(steps,),
            in_specs=[
                stream, stream, halo_spec(1), halo_spec(2), taps_spec, row_spec, row_spec
            ],
            out_specs=[local_spec, pl.BlockSpec((POLES, block), lambda b, *_: (0, b))],
            scratch_shapes=[
                pltpu.VMEM((2, 8, rows + 8, LANES), F32),
                pltpu.VMEM((rows // 8, 8 * 8, LANES), F32),
                pltpu.VMEM((POLES * 8, LANES), F32),
            ],
        ),
        out_shape=[local_shape, jax.ShapeDtypeStruct((POLES, width), F32)],
        name="states",
    )(relative, k_in, v_in, halo, halo, conv_filter, lam_rows, res_rows)

    query = pl.pallas_call(
        functools.partial(query_kernel, rows=rows, genomes=genomes),
        grid_spec=pltpu.PrefetchScalarGridSpec(
            num_scalar_prefetch=1,
            grid=(steps,),
            in_specs=[stream, halo_spec(0), taps_spec],
            out_specs=stream,
            scratch_shapes=[pltpu.VMEM((1, 8, rows + 8, LANES), F32)],
        ),
        out_shape=jax.ShapeDtypeStruct((rows, width), BF16),
        name="query",
        cost_estimate=pl.CostEstimate(
            flops=6 * 10**9, bytes_accessed=5 * rows * width, transcendentals=0
        ),
    )(relative, q_in, halo, conv_filter)

    def end_id(device):
        return jnp.sum((starts <= (device + 1) * rows - 1).astype(jnp.int32))

    def joined(a, b):
        return (end_id(a) == end_id(b)).astype(F32)

    core = index % 2
    half = width // 2

    def mine_of(value):
        return lax.dynamic_slice_in_dim(value, core * half, half, 1)

    lam_mine = mine_of(lam_wide)

    def power(devices):
        return jnp.exp(-lam_mine * (rows * devices).astype(F32))

    def crossed(value, step, only=None):
        pairs = [(i, i ^ step) for i in range(count) if only is None or i // only % 4 in (1, 2)]
        return exchange(value.astype(BF16), pairs).astype(F32)

    one = jnp.int32(1)
    own = mine_of(span)
    got = mine_of(exchange(span, [(i, i ^ 1) for i in range(count)]))
    left = jnp.where(core == 0, own, got)
    right = jnp.where(core == 0, got, own)
    chip = index - core
    total = power(one) * joined(chip, chip + 1) * left + right
    prefix = jnp.zeros_like(total)
    size = 2
    while size * 4 < count or size * 2 == count:
        other = crossed(total, size)
        is_right = (index // size) % 2 == 1
        first = index // size * size
        last = first + size - 1
        into = power(chip - first) * joined(first - 1, chip - 1) * other
        prefix = prefix + jnp.where(is_right, into, 0.0)
        gain = power(jnp.int32(size))
        as_right = gain * joined(first - 1, last) * other + total
        as_left = gain * joined(last, last + size) * total + other
        total = jnp.where(is_right, as_right, as_left)
        size *= 2
    if size * 4 == count:
        block_index = index // size
        for flip, other in (
            (1, crossed(total, size)),
            (3, crossed(total, 3 * size, size)),
            (2, crossed(total, 2 * size)),
        ):
            source = block_index ^ flip
            after = (source + 1) * size
            factor = jnp.where(source < block_index, joined(after - 1, chip - 1), 0.0)
            prefix = prefix + power(jnp.maximum(chip - after, 0)) * factor * other
    second = power(one) * joined(chip - 1, chip) * prefix + left
    mine = jnp.where(core == 0, prefix, second)
    others = jnp.where(core == 0, second, prefix)
    back = exchange(others, [(i, i ^ 1) for i in range(count)])

    groups = width // (2 * LANES)
    flat_spec = pl.BlockSpec((groups // steps, 1, 2 * LANES), lambda b, *_: (b, 0, 0))
    half_spec = pl.BlockSpec((POLES, block), lambda b, *_: (0, b % (steps // 2)))
    return pl.pallas_call(
        functools.partial(gate_kernel, rows=rows, genomes=genomes),
        grid_spec=pltpu.PrefetchScalarGridSpec(
            num_scalar_prefetch=2,
            grid=(steps,),
            in_specs=[local_spec, stream, half_spec, half_spec, flat_spec, flat_spec],
            out_specs=stream,
        ),
        out_shape=jax.ShapeDtypeStruct((rows, width), BF16),
        name="gate",
    )(
        relative, jnp.reshape(core, (1,)).astype(jnp.int32), local, query, mine, back,
        decay_rate.reshape(groups, 1, 2 * LANES), residue.reshape(groups, 1, 2 * LANES),
    )


def solution(mesh):
    in_specs = (
        P(("groups", "ctx"), None),
        P(("groups", "ctx"), None),
        P(("groups", "ctx"), None),
        P(),
        P(),
        P(),
        P("groups"),
    )
    return jax.shard_map(
        per_device, mesh=mesh, in_specs=in_specs, out_specs=P(("groups", "ctx"), None), check_vma=False
    )
```

```python
import functools

import jax
import jax.numpy as jnp
from jax import lax
from jax.experimental import pallas as pl
from jax.experimental.pallas import tpu as pltpu
from jax.sharding import PartitionSpec as P

CPG = 16
POLES = 16
TAPS = 7
LANES = 128
UNIT = 16
GROUP = LANES // CPG
F32 = jnp.float32
BF16 = jnp.bfloat16


def iota(shape, axis):
    return lax.broadcasted_iota(jnp.int32, shape, axis)


def lanes_of(tile):
    if isinstance(tile, int):
        return slice(tile * LANES, (tile + 1) * LANES)
    return pl.ds(pl.multiple_of(tile * LANES, LANES), LANES)


def split(value):
    hi = value.astype(BF16)
    return hi, (value - hi.astype(F32)).astype(BF16)


def any_of(flags):
    return functools.reduce(jnp.logical_or, flags)


def conv_terms(taps, window):
    terms = [taps[j] * window(j) for j in range(TAPS)]
    even = (terms[0] + terms[1]) + (terms[2] + terms[3])
    return even + ((terms[4] + terms[5]) + terms[6])


def short_conv(starts, streams, halo_refs, taps_refs, xs, emit, tiles, rows, genomes):
    count = len(streams)
    cut_above = functools.reduce(
        jnp.maximum, [jnp.where(starts[g] <= 0, starts[g], -rows) for g in range(genomes)]
    )
    halo_kept = iota((8, LANES), 0) - 8 >= cut_above

    def base(tile, _):
        lanes = lanes_of(tile)
        for s in range(count):
            xs[s, tile, :8] = jnp.where(halo_kept, halo_refs[s][:, lanes].astype(F32), 0.0)
            xs[s, tile, 8:] = streams[s][:, lanes].astype(F32)
        taps = [
            [jnp.broadcast_to(taps_refs[s][j : j + 1, lanes], (8, LANES)) for j in range(TAPS)]
            for s in range(count)
        ]
        for r in range(0, rows, UNIT):
            done = []
            for s in range(count):
                for at in (r + 8, r + 16):
                    done.append(
                        conv_terms(
                            taps[s], lambda j, s=s, at=at: xs[s, tile, at - j : at - j + 8]
                        )
                    )
            emit(tile, lanes, r, done)
        return 0

    lax.fori_loop(0, tiles, base, 0)

    def patch(unit):
        first = pl.multiple_of(unit * UNIT, UNIT)
        cuts = []
        for h in range(2):
            at = first + 8 * h + iota((8, LANES), 0)
            cuts.append(
                [
                    any_of([(at >= starts[g]) & (at < starts[g] + j) for g in range(genomes)])
                    for j in range(1, TAPS)
                ]
            )

        def patch_tile(tile, _):
            lanes = lanes_of(tile)
            done = []
            for s in range(count):
                taps = [taps_refs[s][j : j + 1, lanes] for j in range(TAPS)]
                for h in range(2):

                    def window(j, s=s, h=h):
                        moved = xs[s, tile, pl.ds(first + 8 * (h + 1) - j, 8)]
                        return moved if j == 0 else jnp.where(cuts[h][j - 1], 0.0, moved)

                    done.append(conv_terms(taps, window))
            emit(tile, lanes, first, done)
            return 0

        lax.fori_loop(0, tiles, patch_tile, 0)

    for g in range(genomes):
        start = starts[g]
        inside = (start > 0) & (start < rows)
        unit = start // UNIT
        end = jnp.minimum(start + TAPS - 2, rows - 1) // UNIT

        @pl.when(inside)
        def _():
            patch(unit)

        @pl.when(inside & (end != unit))
        def _():
            patch(end)


def exchange_plan(count):
    sizes, size = [], 2
    while size * 4 < count or size * 2 == count:
        sizes.append(size)
        size *= 2
    return sizes, size if size * 4 == count else 0


FLIPS = (1, 3, 2)


def factors(lengths, index, count, rows, genomes):
    starts = [jnp.int32(0)]
    for g in range(1, genomes):
        starts.append(starts[-1] + lengths[g - 1])

    def joined(a, b):
        cut = any_of(
            [(start >= (a + 1) * rows) & (start < (b + 1) * rows) for start in starts]
        )
        return jnp.where(cut, 0.0, 1.0)

    core = lax.rem(index, 2)
    chip = index - core
    out = [(jnp.int32(1), joined(chip, chip + 1))]
    sizes, wide = exchange_plan(count)
    for size in sizes:
        right = lax.rem(lax.div(index, size), 2) == 1
        first = lax.div(index, size) * size
        last = first + size - 1
        out.append((chip - first, jnp.where(right, joined(first - 1, chip - 1), 0.0)))
        out.append((jnp.where(right, size, 0), jnp.where(right, joined(first - 1, last), 1.0)))
        out.append((jnp.where(right, 0, size), jnp.where(right, 1.0, joined(last, last + size))))
    if wide:
        block = lax.div(index, wide)
        for flip in FLIPS:
            source = block ^ flip
            after = (source + 1) * wide
            out.append(
                (
                    jnp.maximum(chip - after, 0),
                    jnp.where(source < block, joined(after - 1, chip - 1), 0.0),
                )
            )
    out.append((jnp.int32(1), joined(chip - 1, chip)))
    return [start - index * rows for start in starts], out, core


def expand_kernel(
    lengths, lam_ref, res_ref, starts_ref, lam_rows, res_rows, factor_ref, lam_mine,
    *, tiles, count, rows, genomes,
):
    index = lax.axis_index("ctx")
    starts, pairs, core = factors(lengths, index, count, rows, genomes)
    for g in range(genomes):
        starts_ref[g] = starts[g]
    parts = []
    for source in (lam_ref, res_ref):
        rest = source[...]
        for _ in range(3):
            part = rest.astype(BF16)
            rest = rest - part.astype(F32)
            parts.append(part)
    parts = jnp.concatenate(parts, 0)
    lams = []
    for pair in range(tiles // 2):
        first = pair * 2 * GROUP
        side = first // LANES * LANES
        shape = (LANES, 2 * LANES)
        pick = iota(shape, 1) // CPG + (first - side) == iota(shape, 0)
        wide = jnp.dot(
            parts[:, side : side + LANES], jnp.where(pick, 1.0, 0.0).astype(BF16),
            preferred_element_type=F32,
        )
        wide = [wide[i * POLES : (i + 1) * POLES] for i in range(6)]
        lam = wide[0] + wide[1] + wide[2]
        res = wide[3] + wide[4] + wide[5]
        half = pl.ds(pair % (tiles // 4) * 2 * LANES, 2 * LANES)
        if pair < tiles // 4:
            lam_mine[:, half] = lam
        else:
            lam_mine[:, half] = jnp.where(core == 0, lam_mine[:, half], lam)
        for t in range(2):
            lam_rows[:, 2 * pair + t, :] = lam[:, lanes_of(t)]
            res_rows[:, 2 * pair + t, :] = res[:, lanes_of(t)]
    for i, (devices, factor) in enumerate(pairs):
        factor_ref[i] = factor * jnp.exp(-lam_mine[...] * (devices * rows).astype(F32))


def states_kernel(
    starts, k_ref, v_ref, k_halo, v_halo, taps_ref, lam_ref, res_ref,
    local_ref, span_ref, xs, mixed, final, *, rows, genomes,
):
    tiles = k_ref.shape[1] // LANES

    def emit(tile, lanes, first, done):
        k0, k1, v0, v1 = (value.astype(BF16).astype(F32) for value in done)
        row = pl.ds(pl.multiple_of(tile * 8, 8), 8)
        mixed[first // 8, row, :] = k0 * v0
        mixed[first // 8 + 1, row, :] = k1 * v1

    short_conv(
        starts, (k_ref, v_ref), (k_halo.at[0], v_halo.at[0]), (taps_ref.at[1], taps_ref.at[2]),
        xs, emit, tiles, rows, genomes,
    )
    decay = [jnp.exp(-lam_ref[n]) for n in range(POLES)]
    weight = [res_ref[n] for n in range(POLES)]

    def one(eight, r, state, keep=None):
        x = mixed[eight, pl.ds(r, tiles, stride=8), :]
        out, sums = [], [None, None]
        for n in range(POLES):
            old = state[n] if keep is None else state[n] * keep
            new = decay[n] * old + x
            term = weight[n] * new
            sums[n % 2] = term if sums[n % 2] is None else sums[n % 2] + term
            out.append(new)
        local_ref[eight, pl.ds(r, tiles, stride=8), :] = sums[0] + sums[1]
        return out

    size = 32

    def block(i, state):
        first = i * size
        cut = any_of(
            [(starts[g] > 0) & (starts[g] >= first) & (starts[g] < first + size) for g in range(genomes)]
        )

        def smooth(state):
            state = list(state)
            for r in range(size):
                state = one(i * (size // 8) + r // 8, r % 8, state)
            return tuple(state)

        def broken(state):
            def step(t, state):
                here = any_of([starts[g] == first + t for g in range(genomes)])
                keep = jnp.where(here, 0.0, 1.0)
                return tuple(one(i * (size // 8) + t // 8, t % 8, list(state), keep))

            return lax.fori_loop(0, size, step, state, unroll=8)

        return lax.cond(cut, broken, smooth, state)

    zero = jnp.zeros((tiles, LANES), F32)
    state = lax.fori_loop(0, rows // size, block, (zero,) * POLES)
    for n in range(POLES):
        final[n * tiles : (n + 1) * tiles, :] = state[n]
    for tile in range(tiles):
        span_ref[:, lanes_of(tile)] = final[pl.ds(tile, POLES, stride=tiles), :]


def query_kernel(starts, q_ref, q_halo, taps_ref, query_ref, xs, *, rows, genomes):
    def emit(tile, lanes, first, done):
        query_ref[pl.ds(first, UNIT), lanes] = jnp.concatenate(done, 0).astype(BF16)

    short_conv(
        starts, (q_ref,), (q_halo.at[0],), (taps_ref.at[0],), xs, emit,
        q_ref.shape[1] // LANES, rows, genomes,
    )


def gate_kernel(
    starts, core_ref, local_ref, query_ref, mine_ref, other_ref, lam_ref, res_ref, out_ref,
    *, rows, genomes,
):
    width = 2 * LANES
    filters = width // CPG
    use_mine = (pl.program_id(0) // (pl.num_programs(0) // 2)) == core_ref[0]
    lane_filter = iota((POLES, width), 1) // CPG
    t = iota((rows, width), 0)
    keep = jnp.logical_not(any_of([(starts[g] >= 0) & (t >= starts[g]) for g in range(genomes)]))
    ahead = jnp.where(keep, (t + 1).astype(F32), 1e9)
    dot = functools.partial(jnp.dot, preferred_element_type=F32)

    def spread(value):
        zero = jnp.zeros((), BF16)
        return jnp.concatenate(
            [jnp.where(lane_filter == f, value, zero) for f in range(filters)], 0
        )

    for group in range(out_ref.shape[1] // width):
        lanes = slice(group * width, (group + 1) * width)
        state = jnp.where(use_mine, mine_ref[:, lanes], other_ref[:, lanes])
        hi, lo = split(state)
        s_hi, s_lo = spread(hi), spread(lo)
        e_hi, e_lo = split(res_ref[group] * jnp.exp(-lam_ref[group] * ahead))
        carried = dot(e_hi, s_hi) + (dot(e_lo, s_hi) + dot(e_hi, s_lo))
        local = jnp.concatenate(
            [
                local_ref[:, (2 * group + t) * 8 : (2 * group + t + 1) * 8, :].reshape(rows, LANES)
                for t in range(2)
            ],
            1,
        )
        filtered = local + carried
        out_ref[:, lanes] = (query_ref[:, lanes].astype(F32) * filtered).astype(BF16)


def exchange(value, pairs):
    return lax.ppermute(value, "ctx", pairs)


def per_device(q_in, k_in, v_in, conv_filter, decay_rate, residue, genome_lengths):
    rows, width = q_in.shape
    tiles = width // LANES
    genomes = genome_lengths.shape[0]
    count = lax.axis_size("ctx")
    index = lax.axis_index("ctx")
    tail = jnp.stack([x[rows - 8 :] for x in (q_in, k_in, v_in)])
    halo = exchange(tail, [(i, i + 1) for i in range(count - 1)])

    block = 8 * LANES
    steps = width // block
    stream = pl.BlockSpec((rows, block), lambda b, *_: (0, b))
    taps_spec = pl.BlockSpec((3, TAPS, block), lambda b, *_: (0, 0, b))
    row_spec = pl.BlockSpec((POLES, 8, LANES), lambda b, *_: (0, b, 0))
    local_spec = pl.BlockSpec((rows // 8, 8 * 8, LANES), lambda b, *_: (0, b, 0))
    local_shape = jax.ShapeDtypeStruct((rows // 8, tiles * 8, LANES), F32)

    def halo_spec(s):
        return pl.BlockSpec((1, 8, block), lambda b, *_: (s, 0, b))

    in_smem = pl.BlockSpec(memory_space=pltpu.SMEM)
    in_vmem = pl.BlockSpec(memory_space=pltpu.VMEM)
    sizes, wide = exchange_plan(count)
    terms = 2 + 3 * len(sizes) + (len(FLIPS) if wide else 0)
    relative, lam_rows, res_rows, factor = pl.pallas_call(
        functools.partial(expand_kernel, tiles=tiles, count=count, rows=rows, genomes=genomes),
        in_specs=[in_smem, in_vmem, in_vmem],
        out_specs=[in_smem] + [in_vmem] * 3,
        out_shape=[
            jax.ShapeDtypeStruct((genomes,), jnp.int32),
            jax.ShapeDtypeStruct((POLES, tiles, LANES), F32),
            jax.ShapeDtypeStruct((POLES, tiles, LANES), F32),
            jax.ShapeDtypeStruct((terms, POLES, width // 2), F32),
        ],
        scratch_shapes=[pltpu.VMEM((POLES, width // 2), F32)],
        name="expand",
        cost_estimate=pl.CostEstimate(flops=10**9, bytes_accessed=10**6, transcendentals=0),
    )(genome_lengths, decay_rate.T, residue.T)

    local, span = pl.pallas_call(
        functools.partial(states_kernel, rows=rows, genomes=genomes),
        grid_spec=pltpu.PrefetchScalarGridSpec(
            num_scalar_prefetch=1,
            grid=(steps,),
            in_specs=[
                stream, stream, halo_spec(1), halo_spec(2), taps_spec, row_spec, row_spec
            ],
            out_specs=[local_spec, pl.BlockSpec((POLES, block), lambda b, *_: (0, b))],
            scratch_shapes=[
                pltpu.VMEM((2, 8, rows + 8, LANES), F32),
                pltpu.VMEM((rows // 8, 8 * 8, LANES), F32),
                pltpu.VMEM((POLES * 8, LANES), F32),
            ],
        ),
        out_shape=[local_shape, jax.ShapeDtypeStruct((POLES, width), F32)],
        name="states",
    )(relative, k_in, v_in, halo, halo, conv_filter, lam_rows, res_rows)

    query = pl.pallas_call(
        functools.partial(query_kernel, rows=rows, genomes=genomes),
        grid_spec=pltpu.PrefetchScalarGridSpec(
            num_scalar_prefetch=1,
            grid=(steps,),
            in_specs=[stream, halo_spec(0), taps_spec],
            out_specs=stream,
            scratch_shapes=[pltpu.VMEM((1, 8, rows + 8, LANES), F32)],
        ),
        out_shape=jax.ShapeDtypeStruct((rows, width), BF16),
        name="query",
        cost_estimate=pl.CostEstimate(
            flops=6 * 10**9, bytes_accessed=5 * rows * width, transcendentals=0
        ),
    )(relative, q_in, halo, conv_filter)

    core = index % 2
    half = width // 2

    def mine_of(value):
        return lax.dynamic_slice_in_dim(value, core * half, half, 1)

    def term(i, value):
        return factor[i] * value

    def crossed(value, step, only=None):
        pairs = [(i, i ^ step) for i in range(count) if only is None or i // only % 4 in (1, 2)]
        return exchange(value, pairs).astype(F32)

    own = mine_of(span)
    got = mine_of(exchange(span, [(i, i ^ 1) for i in range(count)]))
    left = jnp.where(core == 0, own, got)
    right = jnp.where(core == 0, got, own)
    total = term(0, left) + right
    prefix = jnp.zeros_like(total)
    at = 1
    for size in sizes:
        other = crossed(total.astype(BF16), size)
        prefix = prefix + term(at, other)
        total = term(at + 1, other) + term(at + 2, total)
        at += 3
    if wide:
        sent = total.astype(BF16)
        others = [crossed(sent, f * wide, wide if f == 3 else None) for f in FLIPS]
        query, *others = lax.optimization_barrier((query, *others))
        for other in others:
            prefix = prefix + term(at, other)
            at += 1
    second = term(at, prefix) + left
    mine = jnp.where(core == 0, prefix, second)
    others = jnp.where(core == 0, second, prefix)
    back = exchange(others, [(i, i ^ 1) for i in range(count)])

    groups = width // (2 * LANES)
    flat_spec = pl.BlockSpec((groups // steps, 1, 2 * LANES), lambda b, *_: (b, 0, 0))
    half_spec = pl.BlockSpec((POLES, block), lambda b, *_: (0, b % (steps // 2)))
    return pl.pallas_call(
        functools.partial(gate_kernel, rows=rows, genomes=genomes),
        grid_spec=pltpu.PrefetchScalarGridSpec(
            num_scalar_prefetch=2,
            grid=(steps,),
            in_specs=[local_spec, stream, half_spec, half_spec, flat_spec, flat_spec],
            out_specs=stream,
        ),
        out_shape=jax.ShapeDtypeStruct((rows, width), BF16),
        name="gate",
    )(
        relative, jnp.reshape(core, (1,)).astype(jnp.int32), local, query, mine, back,
        decay_rate.reshape(groups, 1, 2 * LANES), residue.reshape(groups, 1, 2 * LANES),
    )


def solution(mesh):
    in_specs = (
        P(("groups", "ctx"), None),
        P(("groups", "ctx"), None),
        P(("groups", "ctx"), None),
        P(),
        P(),
        P(),
        P("groups"),
    )
    return jax.shard_map(
        per_device, mesh=mesh, in_specs=in_specs, out_specs=P(("groups", "ctx"), None), check_vma=False
    )
```

```python
import functools

import jax
import jax.numpy as jnp
from jax import lax
from jax.experimental import pallas as pl
from jax.experimental.pallas import tpu as pltpu
from jax.sharding import PartitionSpec as P

CPG = 16
POLES = 16
TAPS = 7
LANES = 128
UNIT = 16
GROUP = LANES // CPG
F32 = jnp.float32
BF16 = jnp.bfloat16


def iota(shape, axis):
    return lax.broadcasted_iota(jnp.int32, shape, axis)


def lanes_of(tile):
    if isinstance(tile, int):
        return slice(tile * LANES, (tile + 1) * LANES)
    return pl.ds(pl.multiple_of(tile * LANES, LANES), LANES)


def split(value):
    hi = value.astype(BF16)
    return hi, (value - hi.astype(F32)).astype(BF16)


def any_of(flags):
    return functools.reduce(jnp.logical_or, flags)


def conv_terms(taps, window):
    terms = [taps[j] * window(j) for j in range(TAPS)]
    even = (terms[0] + terms[1]) + (terms[2] + terms[3])
    return even + ((terms[4] + terms[5]) + terms[6])


def short_conv(starts, streams, halo_refs, taps_refs, xs, emit, tiles, rows, genomes):
    count = len(streams)
    cut_above = functools.reduce(
        jnp.maximum, [jnp.where(starts[g] <= 0, starts[g], -rows) for g in range(genomes)]
    )
    halo_kept = iota((8, LANES), 0) - 8 >= cut_above

    def base(tile, _):
        lanes = lanes_of(tile)
        for s in range(count):
            xs[s, tile, :8] = jnp.where(halo_kept, halo_refs[s][:, lanes].astype(F32), 0.0)
            xs[s, tile, 8:] = streams[s][:, lanes].astype(F32)
        taps = [
            [jnp.broadcast_to(taps_refs[s][j : j + 1, lanes], (8, LANES)) for j in range(TAPS)]
            for s in range(count)
        ]
        for r in range(0, rows, UNIT):
            done = []
            for s in range(count):
                for at in (r + 8, r + 16):
                    done.append(
                        conv_terms(
                            taps[s], lambda j, s=s, at=at: xs[s, tile, at - j : at - j + 8]
                        )
                    )
            emit(tile, lanes, r, done)
        return 0

    lax.fori_loop(0, tiles, base, 0)

    def patch(unit):
        first = pl.multiple_of(unit * UNIT, UNIT)
        cuts = []
        for h in range(2):
            at = first + 8 * h + iota((8, LANES), 0)
            cuts.append(
                [
                    any_of([(at >= starts[g]) & (at < starts[g] + j) for g in range(genomes)])
                    for j in range(1, TAPS)
                ]
            )

        def patch_tile(tile, _):
            lanes = lanes_of(tile)
            done = []
            for s in range(count):
                taps = [taps_refs[s][j : j + 1, lanes] for j in range(TAPS)]
                for h in range(2):

                    def window(j, s=s, h=h):
                        moved = xs[s, tile, pl.ds(first + 8 * (h + 1) - j, 8)]
                        return moved if j == 0 else jnp.where(cuts[h][j - 1], 0.0, moved)

                    done.append(conv_terms(taps, window))
            emit(tile, lanes, first, done)
            return 0

        lax.fori_loop(0, tiles, patch_tile, 0)

    for g in range(genomes):
        start = starts[g]
        inside = (start > 0) & (start < rows)
        unit = start // UNIT
        end = jnp.minimum(start + TAPS - 2, rows - 1) // UNIT

        @pl.when(inside)
        def _():
            patch(unit)

        @pl.when(inside & (end != unit))
        def _():
            patch(end)


def exchange_plan(count):
    sizes, size = [], 2
    while size * 4 < count or size * 2 == count:
        sizes.append(size)
        size *= 2
    return sizes, size if size * 4 == count else 0


FLIPS = (1, 3, 2)


def factors(lengths, index, count, rows, genomes):
    starts = [jnp.int32(0)]
    for g in range(1, genomes):
        starts.append(starts[-1] + lengths[g - 1])

    def joined(a, b):
        cut = any_of(
            [(start >= (a + 1) * rows) & (start < (b + 1) * rows) for start in starts]
        )
        return jnp.where(cut, 0.0, 1.0)

    core = lax.rem(index, 2)
    chip = index - core
    out = [(jnp.int32(1), joined(chip, chip + 1))]
    sizes, wide = exchange_plan(count)
    for size in sizes:
        right = lax.rem(lax.div(index, size), 2) == 1
        first = lax.div(index, size) * size
        last = first + size - 1
        out.append((chip - first, jnp.where(right, joined(first - 1, chip - 1), 0.0)))
        out.append((jnp.where(right, size, 0), jnp.where(right, joined(first - 1, last), 1.0)))
        out.append((jnp.where(right, 0, size), jnp.where(right, 1.0, joined(last, last + size))))
    if wide:
        block = lax.div(index, wide)
        for flip in FLIPS:
            source = block ^ flip
            after = (source + 1) * wide
            out.append(
                (
                    jnp.maximum(chip - after, 0),
                    jnp.where(source < block, joined(after - 1, chip - 1), 0.0),
                )
            )
    out.append((jnp.int32(1), joined(chip - 1, chip)))
    return [start - index * rows for start in starts], out, core


def expand_kernel(
    lengths, lam_ref, res_ref, starts_ref, lam_rows, res_rows, factor_ref, lam_mine,
    *, tiles, count, rows, genomes,
):
    index = lax.axis_index("ctx")
    starts, pairs, core = factors(lengths, index, count, rows, genomes)
    for g in range(genomes):
        starts_ref[g] = starts[g]
    parts = []
    for source in (lam_ref, res_ref):
        rest = source[...]
        for _ in range(3):
            part = rest.astype(BF16)
            rest = rest - part.astype(F32)
            parts.append(part)
    parts = jnp.concatenate(parts, 0)
    lams = []
    for pair in range(tiles // 2):
        first = pair * 2 * GROUP
        side = first // LANES * LANES
        shape = (LANES, 2 * LANES)
        pick = iota(shape, 1) // CPG + (first - side) == iota(shape, 0)
        wide = jnp.dot(
            parts[:, side : side + LANES], jnp.where(pick, 1.0, 0.0).astype(BF16),
            preferred_element_type=F32,
        )
        wide = [wide[i * POLES : (i + 1) * POLES] for i in range(6)]
        lam = wide[0] + wide[1] + wide[2]
        res = wide[3] + wide[4] + wide[5]
        half = pl.ds(pair % (tiles // 4) * 2 * LANES, 2 * LANES)
        if pair < tiles // 4:
            lam_mine[:, half] = lam
        else:
            lam_mine[:, half] = jnp.where(core == 0, lam_mine[:, half], lam)
        for t in range(2):
            lam_rows[:, 2 * pair + t, :] = lam[:, lanes_of(t)]
            res_rows[:, 2 * pair + t, :] = res[:, lanes_of(t)]
    for i, (devices, factor) in enumerate(pairs):
        factor_ref[i] = factor * jnp.exp(-lam_mine[...] * (devices * rows).astype(F32))


def states_kernel(
    starts, k_ref, v_ref, k_halo, v_halo, taps_ref, lam_ref, res_ref,
    local_ref, span_ref, xs, mixed, final, *, rows, genomes,
):
    tiles = k_ref.shape[1] // LANES

    def emit(tile, lanes, first, done):
        k0, k1, v0, v1 = (value.astype(BF16).astype(F32) for value in done)
        row = pl.ds(pl.multiple_of(tile * 8, 8), 8)
        mixed[first // 8, row, :] = k0 * v0
        mixed[first // 8 + 1, row, :] = k1 * v1

    short_conv(
        starts, (k_ref, v_ref), (k_halo.at[0], v_halo.at[0]), (taps_ref.at[1], taps_ref.at[2]),
        xs, emit, tiles, rows, genomes,
    )
    decay = [jnp.exp(-lam_ref[n]) for n in range(POLES)]
    weight = [res_ref[n] for n in range(POLES)]

    def one(eight, r, state, keep=None):
        x = mixed[eight, pl.ds(r, tiles, stride=8), :]
        out, sums = [], [None, None]
        for n in range(POLES):
            old = state[n] if keep is None else state[n] * keep
            new = decay[n] * old + x
            term = weight[n] * new
            sums[n % 2] = term if sums[n % 2] is None else sums[n % 2] + term
            out.append(new)
        local_ref[eight, pl.ds(r, tiles, stride=8), :] = sums[0] + sums[1]
        return out

    size = 32

    def block(i, state):
        first = i * size
        cut = any_of(
            [(starts[g] > 0) & (starts[g] >= first) & (starts[g] < first + size) for g in range(genomes)]
        )

        def smooth(state):
            state = list(state)
            for r in range(size):
                state = one(i * (size // 8) + r // 8, r % 8, state)
            return tuple(state)

        def broken(state):
            def step(t, state):
                here = any_of([starts[g] == first + t for g in range(genomes)])
                keep = jnp.where(here, 0.0, 1.0)
                return tuple(one(i * (size // 8) + t // 8, t % 8, list(state), keep))

            return lax.fori_loop(0, size, step, state, unroll=8)

        return lax.cond(cut, broken, smooth, state)

    zero = jnp.zeros((tiles, LANES), F32)
    state = lax.fori_loop(0, rows // size, block, (zero,) * POLES)
    for n in range(POLES):
        final[n * tiles : (n + 1) * tiles, :] = state[n]
    for tile in range(tiles):
        span_ref[:, lanes_of(tile)] = final[pl.ds(tile, POLES, stride=tiles), :]


def query_kernel(starts, q_ref, q_halo, taps_ref, query_ref, xs, *, rows, genomes):
    def emit(tile, lanes, first, done):
        query_ref[pl.ds(first, UNIT), lanes] = jnp.concatenate(done, 0).astype(BF16)

    short_conv(
        starts, (q_ref,), (q_halo.at[0],), (taps_ref.at[0],), xs, emit,
        q_ref.shape[1] // LANES, rows, genomes,
    )


def gate_kernel(
    starts, core_ref, local_ref, query_ref, mine_ref, other_ref, lam_ref, res_ref, out_ref,
    *, rows, genomes,
):
    width = 2 * LANES
    filters = width // CPG
    use_mine = (pl.program_id(0) // (pl.num_programs(0) // 2)) == core_ref[0]
    lane_filter = iota((POLES, width), 1) // CPG
    t = iota((rows, width), 0)
    keep = jnp.logical_not(any_of([(starts[g] >= 0) & (t >= starts[g]) for g in range(genomes)]))
    ahead = jnp.where(keep, (t + 1).astype(F32), 1e9)
    dot = functools.partial(jnp.dot, preferred_element_type=F32)

    def spread(value):
        zero = jnp.zeros((), BF16)
        return jnp.concatenate(
            [jnp.where(lane_filter == f, value, zero) for f in range(filters)], 0
        )

    for group in range(out_ref.shape[1] // width):
        lanes = slice(group * width, (group + 1) * width)
        state = jnp.where(use_mine, mine_ref[:, lanes], other_ref[:, lanes])
        hi, lo = split(state)
        s_hi, s_lo = spread(hi), spread(lo)
        e_hi, e_lo = split(res_ref[group] * jnp.exp(-lam_ref[group] * ahead))
        carried = dot(e_hi, s_hi) + (dot(e_lo, s_hi) + dot(e_hi, s_lo))
        local = jnp.concatenate(
            [
                local_ref[:, (2 * group + t) * 8 : (2 * group + t + 1) * 8, :].reshape(rows, LANES)
                for t in range(2)
            ],
            1,
        )
        filtered = local + carried
        out_ref[:, lanes] = (query_ref[:, lanes].astype(F32) * filtered).astype(BF16)


def exchange(value, pairs):
    return lax.ppermute(value, "ctx", pairs)


def in_hbm(value):
    return pltpu.with_memory_space_constraint(value, pltpu.HBM)


def per_device(q_in, k_in, v_in, conv_filter, decay_rate, residue, genome_lengths):
    rows, width = q_in.shape
    tiles = width // LANES
    genomes = genome_lengths.shape[0]
    count = lax.axis_size("ctx")
    index = lax.axis_index("ctx")
    tail = jnp.stack([x[rows - 8 :] for x in (q_in, k_in, v_in)])
    halo = exchange(tail, [(i, i + 1) for i in range(count - 1)])

    block = 8 * LANES
    steps = width // block
    stream = pl.BlockSpec((rows, block), lambda b, *_: (0, b))
    taps_spec = pl.BlockSpec((3, TAPS, block), lambda b, *_: (0, 0, b))
    row_spec = pl.BlockSpec((POLES, 8, LANES), lambda b, *_: (0, b, 0))
    local_spec = pl.BlockSpec((rows // 8, 8 * 8, LANES), lambda b, *_: (0, b, 0))
    local_shape = pltpu.HBM((rows // 8, tiles * 8, LANES), F32)

    def halo_spec(s):
        return pl.BlockSpec((1, 8, block), lambda b, *_: (s, 0, b))

    in_smem = pl.BlockSpec(memory_space=pltpu.SMEM)
    in_vmem = pl.BlockSpec(memory_space=pltpu.VMEM)
    sizes, wide = exchange_plan(count)
    terms = 2 + 3 * len(sizes) + (len(FLIPS) if wide else 0)
    relative, lam_rows, res_rows, factor = pl.pallas_call(
        functools.partial(expand_kernel, tiles=tiles, count=count, rows=rows, genomes=genomes),
        in_specs=[in_smem, in_vmem, in_vmem],
        out_specs=[in_smem] + [in_vmem] * 3,
        out_shape=[
            jax.ShapeDtypeStruct((genomes,), jnp.int32),
            jax.ShapeDtypeStruct((POLES, tiles, LANES), F32),
            jax.ShapeDtypeStruct((POLES, tiles, LANES), F32),
            jax.ShapeDtypeStruct((terms, POLES, width // 2), F32),
        ],
        scratch_shapes=[pltpu.VMEM((POLES, width // 2), F32)],
        name="expand",
        compiler_params=pltpu.CompilerParams(vmem_limit_bytes=16 << 20),
        cost_estimate=pl.CostEstimate(flops=10**9, bytes_accessed=10**6, transcendentals=0),
    )(genome_lengths, in_hbm(decay_rate.T), in_hbm(residue.T))

    local, span = pl.pallas_call(
        functools.partial(states_kernel, rows=rows, genomes=genomes),
        grid_spec=pltpu.PrefetchScalarGridSpec(
            num_scalar_prefetch=1,
            grid=(steps,),
            in_specs=[
                stream, stream, halo_spec(1), halo_spec(2), taps_spec, row_spec, row_spec
            ],
            out_specs=[local_spec, pl.BlockSpec((POLES, block), lambda b, *_: (0, b))],
            scratch_shapes=[
                pltpu.VMEM((2, 8, rows + 8, LANES), F32),
                pltpu.VMEM((rows // 8, 8 * 8, LANES), F32),
                pltpu.VMEM((POLES * 8, LANES), F32),
            ],
        ),
        out_shape=[local_shape, jax.ShapeDtypeStruct((POLES, width), F32)],
        name="states",
        compiler_params=pltpu.CompilerParams(vmem_limit_bytes=40 << 20),
    )(relative, k_in, v_in, halo, halo, in_hbm(conv_filter), lam_rows, res_rows)

    query = pl.pallas_call(
        functools.partial(query_kernel, rows=rows, genomes=genomes),
        grid_spec=pltpu.PrefetchScalarGridSpec(
            num_scalar_prefetch=1,
            grid=(steps,),
            in_specs=[stream, halo_spec(0), taps_spec],
            out_specs=stream,
            scratch_shapes=[pltpu.VMEM((1, 8, rows + 8, LANES), F32)],
        ),
        out_shape=jax.ShapeDtypeStruct((rows, width), BF16),
        name="query",
        compiler_params=pltpu.CompilerParams(vmem_limit_bytes=16 << 20),
        cost_estimate=pl.CostEstimate(
            flops=6 * 10**9, bytes_accessed=5 * rows * width, transcendentals=0
        ),
    )(relative, in_hbm(q_in), halo, in_hbm(conv_filter))

    core = index % 2
    half = width // 2

    def mine_of(value):
        return lax.dynamic_slice_in_dim(value, core * half, half, 1)

    def term(i, value):
        return factor[i] * value

    def crossed(value, step, only=None):
        pairs = [(i, i ^ step) for i in range(count) if only is None or i // only % 4 in (1, 2)]
        return exchange(value, pairs).astype(F32)

    own = mine_of(span)
    got = mine_of(exchange(span, [(i, i ^ 1) for i in range(count)]))
    left = jnp.where(core == 0, own, got)
    right = jnp.where(core == 0, got, own)
    total = term(0, left) + right
    prefix = jnp.zeros_like(total)
    at = 1
    for size in sizes:
        other = crossed(total.astype(BF16), size)
        prefix = prefix + term(at, other)
        total = term(at + 1, other) + term(at + 2, total)
        at += 3
    if wide:
        sent = total.astype(BF16)
        others = [crossed(sent, f * wide, wide if f == 3 else None) for f in FLIPS]
        query, *others = lax.optimization_barrier((query, *others))
        for other in others:
            prefix = prefix + term(at, other)
            at += 1
    second = term(at, prefix) + left
    mine = jnp.where(core == 0, prefix, second)
    others = jnp.where(core == 0, second, prefix)
    back = exchange(others, [(i, i ^ 1) for i in range(count)])

    groups = width // (2 * LANES)
    flat_spec = pl.BlockSpec((groups // steps, 1, 2 * LANES), lambda b, *_: (b, 0, 0))
    half_spec = pl.BlockSpec((POLES, block), lambda b, *_: (0, b % (steps // 2)))
    return pl.pallas_call(
        functools.partial(gate_kernel, rows=rows, genomes=genomes),
        grid_spec=pltpu.PrefetchScalarGridSpec(
            num_scalar_prefetch=2,
            grid=(steps,),
            in_specs=[local_spec, stream, half_spec, half_spec, flat_spec, flat_spec],
            out_specs=stream,
        ),
        out_shape=jax.ShapeDtypeStruct((rows, width), BF16),
        name="gate",
        compiler_params=pltpu.CompilerParams(vmem_limit_bytes=40 << 20),
    )(
        relative, jnp.reshape(core, (1,)).astype(jnp.int32), local, query, mine, back,
        decay_rate.reshape(groups, 1, 2 * LANES), residue.reshape(groups, 1, 2 * LANES),
    )


def solution(mesh):
    in_specs = (
        P(("groups", "ctx"), None),
        P(("groups", "ctx"), None),
        P(("groups", "ctx"), None),
        P(),
        P(),
        P(),
        P("groups"),
    )
    return jax.shard_map(
        per_device, mesh=mesh, in_specs=in_specs, out_specs=P(("groups", "ctx"), None), check_vma=False
    )
```

```python
import functools

import jax
import jax.numpy as jnp
from jax import lax
from jax.experimental import pallas as pl
from jax.experimental.pallas import tpu as pltpu
from jax.sharding import PartitionSpec as P

CPG = 16
POLES = 16
TAPS = 7
LANES = 128
UNIT = 16
GROUP = LANES // CPG
F32 = jnp.float32
BF16 = jnp.bfloat16


def iota(shape, axis):
    return lax.broadcasted_iota(jnp.int32, shape, axis)


def lanes_of(tile):
    if isinstance(tile, int):
        return slice(tile * LANES, (tile + 1) * LANES)
    return pl.ds(pl.multiple_of(tile * LANES, LANES), LANES)


def split(value):
    hi = value.astype(BF16)
    return hi, (value - hi.astype(F32)).astype(BF16)


def any_of(flags):
    return functools.reduce(jnp.logical_or, flags)


def conv_terms(taps, window):
    terms = [taps[j] * window(j) for j in range(TAPS)]
    even = (terms[0] + terms[1]) + (terms[2] + terms[3])
    return even + ((terms[4] + terms[5]) + terms[6])


def short_conv(starts, streams, halo_refs, taps_refs, xs, emit, tiles, rows, genomes):
    count = len(streams)
    cut_above = functools.reduce(
        jnp.maximum, [jnp.where(starts[g] <= 0, starts[g], -rows) for g in range(genomes)]
    )
    halo_kept = iota((8, LANES), 0) - 8 >= cut_above

    def base(tile, _):
        lanes = lanes_of(tile)
        for s in range(count):
            xs[s, tile, :8] = jnp.where(halo_kept, halo_refs[s][:, lanes].astype(F32), 0.0)
            xs[s, tile, 8:] = streams[s][:, lanes].astype(F32)
        taps = [
            [jnp.broadcast_to(taps_refs[s][j : j + 1, lanes], (8, LANES)) for j in range(TAPS)]
            for s in range(count)
        ]
        for r in range(0, rows, UNIT):
            done = []
            for s in range(count):
                for at in (r + 8, r + 16):
                    done.append(
                        conv_terms(
                            taps[s], lambda j, s=s, at=at: xs[s, tile, at - j : at - j + 8]
                        )
                    )
            emit(tile, lanes, r, done)
        return 0

    lax.fori_loop(0, tiles, base, 0)

    def patch(unit):
        first = pl.multiple_of(unit * UNIT, UNIT)
        cuts = []
        for h in range(2):
            at = first + 8 * h + iota((8, LANES), 0)
            cuts.append(
                [
                    any_of([(at >= starts[g]) & (at < starts[g] + j) for g in range(genomes)])
                    for j in range(1, TAPS)
                ]
            )

        def patch_tile(tile, _):
            lanes = lanes_of(tile)
            done = []
            for s in range(count):
                taps = [taps_refs[s][j : j + 1, lanes] for j in range(TAPS)]
                for h in range(2):

                    def window(j, s=s, h=h):
                        moved = xs[s, tile, pl.ds(first + 8 * (h + 1) - j, 8)]
                        return moved if j == 0 else jnp.where(cuts[h][j - 1], 0.0, moved)

                    done.append(conv_terms(taps, window))
            emit(tile, lanes, first, done)
            return 0

        lax.fori_loop(0, tiles, patch_tile, 0)

    for g in range(genomes):
        start = starts[g]
        inside = (start > 0) & (start < rows)
        unit = start // UNIT
        end = jnp.minimum(start + TAPS - 2, rows - 1) // UNIT

        @pl.when(inside)
        def _():
            patch(unit)

        @pl.when(inside & (end != unit))
        def _():
            patch(end)


def exchange_plan(count):
    sizes, size = [], 2
    while size * 4 < count or size * 2 == count:
        sizes.append(size)
        size *= 2
    return sizes, size if size * 4 == count else 0


def factors(lengths, index, count, rows, genomes):
    starts = [jnp.int32(0)]
    for g in range(1, genomes):
        starts.append(starts[-1] + lengths[g - 1])

    def joined(a, b):
        cut = any_of(
            [(start >= (a + 1) * rows) & (start < (b + 1) * rows) for start in starts]
        )
        return jnp.where(cut, 0.0, 1.0)

    core = lax.rem(index, 2)
    chip = index - core
    out = [(jnp.int32(1), joined(chip, chip + 1))]
    sizes, wide = exchange_plan(count)
    for size in sizes:
        right = lax.rem(lax.div(index, size), 2) == 1
        first = lax.div(index, size) * size
        last = first + size - 1
        out.append((chip - first, jnp.where(right, joined(first - 1, chip - 1), 0.0)))
        out.append((jnp.where(right, size, 0), jnp.where(right, joined(first - 1, last), 1.0)))
        out.append((jnp.where(right, 0, size), jnp.where(right, 1.0, joined(last, last + size))))
    if wide:
        block = lax.div(index, wide)
        for source in (block - 1, block ^ 2):
            after = (source + 1) * wide
            out.append(
                (
                    jnp.maximum(chip - after, 0),
                    jnp.where(
                        (source >= 0) & (source < block), joined(after - 1, chip - 1), 0.0
                    ),
                )
            )
    out.append((jnp.int32(1), joined(chip - 1, chip)))
    return [start - index * rows for start in starts], out, core


def expand_kernel(
    lengths, lam_ref, res_ref, starts_ref, lam_rows, res_rows, factor_ref, lam_mine,
    *, tiles, count, rows, genomes,
):
    index = lax.axis_index("ctx")
    starts, pairs, core = factors(lengths, index, count, rows, genomes)
    for g in range(genomes):
        starts_ref[g] = starts[g]
    parts = []
    for source in (lam_ref, res_ref):
        rest = source[...]
        for _ in range(3):
            part = rest.astype(BF16)
            rest = rest - part.astype(F32)
            parts.append(part)
    parts = jnp.concatenate(parts, 0)
    lams = []
    for pair in range(tiles // 2):
        first = pair * 2 * GROUP
        side = first // LANES * LANES
        shape = (LANES, 2 * LANES)
        pick = iota(shape, 1) // CPG + (first - side) == iota(shape, 0)
        wide = jnp.dot(
            parts[:, side : side + LANES], jnp.where(pick, 1.0, 0.0).astype(BF16),
            preferred_element_type=F32,
        )
        wide = [wide[i * POLES : (i + 1) * POLES] for i in range(6)]
        lam = wide[0] + wide[1] + wide[2]
        res = wide[3] + wide[4] + wide[5]
        half = pl.ds(pair % (tiles // 4) * 2 * LANES, 2 * LANES)
        if pair < tiles // 4:
            lam_mine[:, half] = lam
        else:
            lam_mine[:, half] = jnp.where(core == 0, lam_mine[:, half], lam)
        for t in range(2):
            lam_rows[:, 2 * pair + t, :] = lam[:, lanes_of(t)]
            res_rows[:, 2 * pair + t, :] = res[:, lanes_of(t)]
    for i, (devices, factor) in enumerate(pairs):
        factor_ref[i] = factor * jnp.exp(-lam_mine[...] * (devices * rows).astype(F32))


def tail_kernel(q_ref, k_ref, v_ref, out_ref):
    for s, ref in enumerate((q_ref, k_ref, v_ref)):
        out_ref[s] = ref[...]


def states_kernel(
    starts, k_ref, v_ref, k_halo, v_halo, taps_ref, lam_ref, res_ref,
    local_ref, span_ref, xs, mixed, final, *, rows, genomes,
):
    tiles = k_ref.shape[1] // LANES

    def emit(tile, lanes, first, done):
        k0, k1, v0, v1 = (value.astype(BF16).astype(F32) for value in done)
        row = pl.ds(pl.multiple_of(tile * 8, 8), 8)
        mixed[first // 8, row, :] = k0 * v0
        mixed[first // 8 + 1, row, :] = k1 * v1

    short_conv(
        starts, (k_ref, v_ref), (k_halo.at[0], v_halo.at[0]), (taps_ref.at[1], taps_ref.at[2]),
        xs, emit, tiles, rows, genomes,
    )
    decay = [jnp.exp(-lam_ref[n]) for n in range(POLES)]
    weight = [res_ref[n] for n in range(POLES)]

    def one(eight, r, state, keep=None):
        x = mixed[eight, pl.ds(r, tiles, stride=8), :]
        out, sums = [], [None, None]
        for n in range(POLES):
            old = state[n] if keep is None else state[n] * keep
            new = decay[n] * old + x
            term = weight[n] * new
            sums[n % 2] = term if sums[n % 2] is None else sums[n % 2] + term
            out.append(new)
        local_ref[eight, pl.ds(r, tiles, stride=8), :] = sums[0] + sums[1]
        return out

    size = 32

    def block(i, state):
        first = i * size
        cut = any_of(
            [(starts[g] > 0) & (starts[g] >= first) & (starts[g] < first + size) for g in range(genomes)]
        )

        def smooth(state):
            state = list(state)
            for r in range(size):
                state = one(i * (size // 8) + r // 8, r % 8, state)
            return tuple(state)

        def broken(state):
            def step(t, state):
                here = any_of([starts[g] == first + t for g in range(genomes)])
                keep = jnp.where(here, 0.0, 1.0)
                return tuple(one(i * (size // 8) + t // 8, t % 8, list(state), keep))

            return lax.fori_loop(0, size, step, state, unroll=8)

        return lax.cond(cut, broken, smooth, state)

    zero = jnp.zeros((tiles, LANES), F32)
    state = lax.fori_loop(0, rows // size, block, (zero,) * POLES)
    for n in range(POLES):
        final[n * tiles : (n + 1) * tiles, :] = state[n]
    for tile in range(tiles):
        span_ref[:, lanes_of(tile)] = final[pl.ds(tile, POLES, stride=tiles), :]


def query_kernel(starts, q_ref, q_halo, taps_ref, query_ref, xs, *, rows, genomes):
    def emit(tile, lanes, first, done):
        query_ref[pl.ds(first, UNIT), lanes] = jnp.concatenate(done, 0).astype(BF16)

    short_conv(
        starts, (q_ref,), (q_halo.at[0],), (taps_ref.at[0],), xs, emit,
        q_ref.shape[1] // LANES, rows, genomes,
    )


def gate_kernel(
    starts, core_ref, local_ref, query_ref, mine_ref, other_ref, lam_ref, res_ref, out_ref,
    *, rows, genomes,
):
    width = 2 * LANES
    filters = width // CPG
    use_mine = (pl.program_id(0) // (pl.num_programs(0) // 2)) == core_ref[0]
    lane_filter = iota((POLES, width), 1) // CPG
    t = iota((rows, width), 0)
    keep = jnp.logical_not(any_of([(starts[g] >= 0) & (t >= starts[g]) for g in range(genomes)]))
    ahead = jnp.where(keep, (t + 1).astype(F32), 1e9)
    dot = functools.partial(jnp.dot, preferred_element_type=F32)

    def spread(value):
        zero = jnp.zeros((), BF16)
        return jnp.concatenate(
            [jnp.where(lane_filter == f, value, zero) for f in range(filters)], 0
        )

    for group in range(out_ref.shape[1] // width):
        lanes = slice(group * width, (group + 1) * width)
        state = jnp.where(use_mine, mine_ref[:, lanes], other_ref[:, lanes])
        hi, lo = split(state)
        s_hi, s_lo = spread(hi), spread(lo)
        e_hi, e_lo = split(res_ref[group] * jnp.exp(-lam_ref[group] * ahead))
        carried = dot(e_hi, s_hi) + (dot(e_lo, s_hi) + dot(e_hi, s_lo))
        local = jnp.concatenate(
            [
                local_ref[:, (2 * group + t) * 8 : (2 * group + t + 1) * 8, :].reshape(rows, LANES)
                for t in range(2)
            ],
            1,
        )
        filtered = local + carried
        out_ref[:, lanes] = (query_ref[:, lanes].astype(F32) * filtered).astype(BF16)


def exchange(value, pairs):
    return lax.ppermute(value, "ctx", pairs)


def in_hbm(value):
    return pltpu.with_memory_space_constraint(value, pltpu.HBM)


def per_device(q_in, k_in, v_in, conv_filter, decay_rate, residue, genome_lengths):
    rows, width = q_in.shape
    tiles = width // LANES
    genomes = genome_lengths.shape[0]
    count = lax.axis_size("ctx")
    index = lax.axis_index("ctx")
    tail = pl.pallas_call(
        tail_kernel,
        grid=(1,),
        in_specs=[pl.BlockSpec((8, width), lambda i: (rows // 8 - 1, 0))] * 3,
        out_specs=pl.BlockSpec((3, 8, width), lambda i: (0, 0, 0)),
        out_shape=jax.ShapeDtypeStruct((3, 8, width), BF16),
        name="tail",
        compiler_params=pltpu.CompilerParams(vmem_limit_bytes=16 << 20),
    )(in_hbm(q_in), in_hbm(k_in), in_hbm(v_in))
    halo = exchange(tail, [(i, i + 1) for i in range(count - 1)])

    block = 8 * LANES
    steps = width // block
    stream = pl.BlockSpec((rows, block), lambda b, *_: (0, b))
    taps_spec = pl.BlockSpec((3, TAPS, block), lambda b, *_: (0, 0, b))
    row_spec = pl.BlockSpec((POLES, 8, LANES), lambda b, *_: (0, b, 0))
    local_spec = pl.BlockSpec((rows // 8, 8 * 8, LANES), lambda b, *_: (0, b, 0))
    local_shape = pltpu.HBM((rows // 8, tiles * 8, LANES), F32)

    def halo_spec(s):
        return pl.BlockSpec((1, 8, block), lambda b, *_: (s, 0, b))

    in_smem = pl.BlockSpec(memory_space=pltpu.SMEM)
    in_vmem = pl.BlockSpec(memory_space=pltpu.VMEM)
    sizes, wide = exchange_plan(count)
    terms = 2 + 3 * len(sizes) + (2 if wide else 0)
    relative, lam_rows, res_rows, factor = pl.pallas_call(
        functools.partial(expand_kernel, tiles=tiles, count=count, rows=rows, genomes=genomes),
        in_specs=[in_smem, in_vmem, in_vmem],
        out_specs=[in_smem] + [in_vmem] * 3,
        out_shape=[
            jax.ShapeDtypeStruct((genomes,), jnp.int32),
            jax.ShapeDtypeStruct((POLES, tiles, LANES), F32),
            jax.ShapeDtypeStruct((POLES, tiles, LANES), F32),
            jax.ShapeDtypeStruct((terms, POLES, width // 2), F32),
        ],
        scratch_shapes=[pltpu.VMEM((POLES, width // 2), F32)],
        name="expand",
        compiler_params=pltpu.CompilerParams(vmem_limit_bytes=16 << 20),
        cost_estimate=pl.CostEstimate(flops=10**9, bytes_accessed=10**6, transcendentals=0),
    )(in_hbm(genome_lengths), in_hbm(decay_rate.T), in_hbm(residue.T))

    local, span = pl.pallas_call(
        functools.partial(states_kernel, rows=rows, genomes=genomes),
        grid_spec=pltpu.PrefetchScalarGridSpec(
            num_scalar_prefetch=1,
            grid=(steps,),
            in_specs=[
                stream, stream, halo_spec(1), halo_spec(2), taps_spec, row_spec, row_spec
            ],
            out_specs=[local_spec, pl.BlockSpec((POLES, block), lambda b, *_: (0, b))],
            scratch_shapes=[
                pltpu.VMEM((2, 8, rows + 8, LANES), F32),
                pltpu.VMEM((rows // 8, 8 * 8, LANES), F32),
                pltpu.VMEM((POLES * 8, LANES), F32),
            ],
        ),
        out_shape=[local_shape, jax.ShapeDtypeStruct((POLES, width), F32)],
        name="states",
        compiler_params=pltpu.CompilerParams(vmem_limit_bytes=40 << 20),
    )(relative, k_in, v_in, halo, halo, in_hbm(conv_filter), lam_rows, res_rows)

    query = pl.pallas_call(
        functools.partial(query_kernel, rows=rows, genomes=genomes),
        grid_spec=pltpu.PrefetchScalarGridSpec(
            num_scalar_prefetch=1,
            grid=(steps,),
            in_specs=[stream, halo_spec(0), taps_spec],
            out_specs=stream,
            scratch_shapes=[pltpu.VMEM((1, 8, rows + 8, LANES), F32)],
        ),
        out_shape=jax.ShapeDtypeStruct((rows, width), BF16),
        name="query",
        compiler_params=pltpu.CompilerParams(vmem_limit_bytes=16 << 20),
        cost_estimate=pl.CostEstimate(
            flops=6 * 10**9, bytes_accessed=5 * rows * width, transcendentals=0
        ),
    )(relative, in_hbm(q_in), halo, in_hbm(conv_filter))

    core = index % 2
    half = width // 2

    def mine_of(value):
        return lax.dynamic_slice_in_dim(value, core * half, half, 1)

    def term(i, value):
        return factor[i] * value

    def crossed(value, step):
        return exchange(value, [(i, i ^ step) for i in range(count)]).astype(F32)

    own = mine_of(span)
    got = mine_of(exchange(span, [(i, i ^ 1) for i in range(count)]))
    left = jnp.where(core == 0, own, got)
    right = jnp.where(core == 0, got, own)
    total = term(0, left) + right
    prefix = jnp.zeros_like(total)
    at = 1
    for size in sizes:
        other = crossed(total.astype(BF16), size)
        prefix = prefix + term(at, other)
        total = term(at + 1, other) + term(at + 2, total)
        at += 3
    if wide:
        sent = total.astype(BF16)
        others = [
            exchange(sent, [(i, i + wide) for i in range(count - wide)]).astype(F32),
            crossed(sent, 2 * wide),
        ]
        query, *others = lax.optimization_barrier((query, *others))
        for other in others:
            prefix = prefix + term(at, other)
            at += 1
    second = term(at, prefix) + left
    mine = jnp.where(core == 0, prefix, second)
    others = jnp.where(core == 0, second, prefix)
    back = exchange(others, [(i, i ^ 1) for i in range(count)])

    groups = width // (2 * LANES)
    flat_spec = pl.BlockSpec((groups // steps, 1, 2 * LANES), lambda b, *_: (b, 0, 0))
    half_spec = pl.BlockSpec((POLES, block), lambda b, *_: (0, b % (steps // 2)))
    return pl.pallas_call(
        functools.partial(gate_kernel, rows=rows, genomes=genomes),
        grid_spec=pltpu.PrefetchScalarGridSpec(
            num_scalar_prefetch=2,
            grid=(steps,),
            in_specs=[local_spec, stream, half_spec, half_spec, flat_spec, flat_spec],
            out_specs=stream,
        ),
        out_shape=jax.ShapeDtypeStruct((rows, width), BF16),
        name="gate",
        compiler_params=pltpu.CompilerParams(vmem_limit_bytes=40 << 20),
    )(
        relative, jnp.reshape(core, (1,)).astype(jnp.int32), local, query, mine, back,
        decay_rate.reshape(groups, 1, 2 * LANES), residue.reshape(groups, 1, 2 * LANES),
    )


def solution(mesh):
    in_specs = (
        P(("groups", "ctx"), None),
        P(("groups", "ctx"), None),
        P(("groups", "ctx"), None),
        P(),
        P(),
        P(),
        P("groups"),
    )
    return jax.shard_map(
        per_device, mesh=mesh, in_specs=in_specs, out_specs=P(("groups", "ctx"), None), check_vma=False
    )
```
